256 devices in a mesh: expert: 64 (over y, z, core), tensor: 4 (over x).
Axes of the slice: x: 4, y: 4, z: 8, core: 2. Of those that a mesh axis runs over, the one named last changes fastest.
Arguments:
- activations: bfloat16 [32768, 4096], P(('expert', 'tensor')), may hold values from -6 to 6
- out_grad: bfloat16 [32768, 4096], P(('expert', 'tensor')), may hold values from -6 to 6
- expert_ids: int32 [32768, 1], P('expert'), may hold values from 0 to 63; in each aligned block of 128 rows (0 to 127, 128 to 255, ...) at most 3 rows name the same one
- gate_weights: bfloat16 [32768, 1], P('expert'), may hold values from 0.049804688 to 1
- weight_in: bfloat16 [64, 4096, 1536], P('expert', None, 'tensor'), may hold values from -0.09375 to 0.09375
- weight_out: bfloat16 [64, 1536, 4096], P('expert', 'tensor'), may hold values from -0.15625 to 0.15625
Outputs:
- grad_in: bfloat16 [32768, 4096], P(('expert', 'tensor'))
- grad_gates: float32 [32768, 1], P(('expert', 'tensor'))
- grad_weight_out: bfloat16 [64, 1536, 4096], P('expert', 'tensor')
The draws below stay inside these ranges and needn't reach their ends.
Inputs may be any that keep to these rules, and one draw needn't show every extreme that they name: `expert_ids`: each token names 1 different experts. Among the 128 tokens of one device (aligned blocks of rows) no expert is named by more than 3 tokens, and in every draw some expert is named by exactly 3 tokens of some device.
All inputs are finite; a program needn't handle non-finite values.
Results may differ from the reference program's by a relative error of at most 0.013.
Values may be sent and summed in bfloat16 or wider, within the bound.
No kernel may reach another device: no remote copies, remote signals or barrier semaphores. Data moves between devices by JAX's collectives and lax.ppermute only.
A program may use at most 128 MiB of HBM per device.

```python
import math
import jax
import jax.numpy as jnp
import numpy as np
from jax import lax

D = 4096
FF = 1536
PICKS = 1
EXPERTS = 64
TOK_DEV = 128
CAP = 3
TOKENS = 32768
N_TENSOR = 4


def level_of(key, extent, cuts, smallest, high):
    def one(dim, shards_of):
        heights = jax.random.uniform(jax.random.fold_in(jax.random.fold_in(key, 6), dim), (shards_of,), jnp.float32, smallest / len(cuts), high / len(cuts))
        return jnp.repeat(jnp.exp(heights), extent[dim] // shards_of).reshape((-1,) + (1,) * (len(extent) - dim - 1))

    gain = one(*cuts[0])
    for cut in cuts[1:]:
        gain = gain * one(*cut)
    return gain


def assign_block(own_key, own, number, rows, number_of, top, most, skew):
    ranking = jax.random.permutation(own_key, number_of)
    packed, common = shares(number_of, rows * top, most, skew, True), shares(number_of, rows * top, most, skew, False)
    places = jnp.arange(number_of)

    def named(sizes, turn):
        used = int((sizes > 0).sum())
        fixed = max(1, used // 4)
        moved = fixed + (places - fixed + turn * (used - fixed)) % max(1, number_of - fixed)
        return jnp.zeros((number_of,), jnp.int32).at[ranking[jnp.where(places < fixed, places, moved)]].set(jnp.asarray(sizes, jnp.int32))

    sizes = jnp.where(number % 4 == 0, named(packed, number // 4), named(common, number - number // 4 - 1))
    mixed = jax.random.permutation(jax.random.fold_in(own, 3), number_of)
    donor, receiver = mixed[0:number_of // 2 * 2:2], mixed[1:number_of // 2 * 2:2]
    slack = jnp.minimum(sizes[donor] - 1, most - sizes[receiver]) // 2
    slack = jnp.where((donor == ranking[0]) | (receiver == ranking[0]) | (sizes[receiver] == 0), 0, jnp.maximum(slack, 0))
    moved = jax.random.randint(jax.random.fold_in(own, 4), (number_of // 2,), 0, 1 << 20) % (slack + 1)
    sizes = sizes.at[donor].add(-moved).at[receiver].add(moved)
    members = jnp.searchsorted(jnp.cumsum(sizes), jnp.arange(rows * top), side="right").astype(jnp.int32)
    listing = members.reshape(top, rows).T
    listing = listing[jax.random.permutation(jax.random.fold_in(own, 1), rows)]
    turn = jax.random.randint(jax.random.fold_in(own, 2), (rows, 1), 0, top)
    return jnp.take_along_axis(listing, (jnp.arange(top)[None, :] + turn) % top, axis=1)


def shares(count, total, limit, skew, full):
    loads = [(1 << 20) // math.isqrt(rank ** skew) + 1 for rank in range(1, count + 1)]
    largest = limit if full else min(limit, max(-(-total // count), total * loads[0] // sum(loads)))
    least = 1 if total - largest >= count - 1 else 0
    holding, surplus = [largest] + [least] * (count - 1), total - largest - least * (count - 1)
    while surplus > 0:
        free = [i for i in range(1, count) if holding[i] < largest] or [i for i in range(1, count) if holding[i] < limit]
        pool, budget = sum([loads[i] for i in free]), surplus
        for i in free:
            more = min(limit - holding[i], max(1, budget * loads[i] // pool), surplus)
            holding[i] = holding[i] + more
            surplus = surplus - more
    return np.array(holding)


def scatter_about(stream_key, shape, spread, most, cuts=(), held_as=jnp.bfloat16):
    array = jax.random.normal(stream_key, shape, jnp.float32) * spread
    if len(cuts) > 0:
        array = level_of(stream_key, shape, cuts, -0.22, 0.18) * array
    return jnp.clip(array, min=-most, max=most).astype(held_as)


def setup_inputs(seed: int = 0) -> dict:
    streams_of = jax.random.split(jax.random.key(seed), 7)
    activations = scatter_about(streams_of[0], (TOKENS, D), 1.0, 6.0, ((0, 256),))
    out_grad = scatter_about(streams_of[1], (TOKENS, D), 1.0, 6.0, ((0, 256),))
    expert_ids_keys = jax.random.split(jax.random.fold_in(streams_of[2], 1), TOKENS // TOK_DEV)
    expert_ids_turns = jax.random.permutation(jax.random.fold_in(streams_of[2], 3), TOKENS // TOK_DEV)
    expert_ids = jax.vmap(lambda own, number: assign_block(jax.random.fold_in(streams_of[2], 2), own, number, TOK_DEV, EXPERTS, PICKS, CAP, 1))(expert_ids_keys, expert_ids_turns).reshape((TOKENS, PICKS))
    gate_weights = jnp.clip(jnp.exp(math.log(1.0) - 2.9996462 * jax.random.uniform(streams_of[3], (TOKENS, PICKS), jnp.float32) ** level_of(streams_of[3], (TOKENS, PICKS), ((0, 64),), -0.2, 0.2)), 0.049804688, 1.0).astype(jnp.bfloat16)
    weight_in = scatter_about(streams_of[4], (EXPERTS, D, FF), D ** -0.5, 0.09375, ((0, 64), (2, 4)))
    weight_out = scatter_about(streams_of[5], (EXPERTS, FF, D), FF ** -0.5, 0.15625, ((0, 64), (1, 4)))
    return {"activations": activations, "out_grad": out_grad, "expert_ids": expert_ids, "gate_weights": gate_weights, "weight_in": weight_in, "weight_out": weight_out}


ROOT_HALF = 0.7071067811865476
INV_ROOT_TAU = 0.3989422804014327


def slot_places(expert_ids, num_blocks, capacity, num_experts):
    row_count = expert_ids.shape[0]
    block_rows = row_count // num_blocks
    matches = (expert_ids[:, :, None] == jnp.arange(num_experts, dtype=jnp.int32)).astype(jnp.int32)
    chosen = jnp.sum(matches, axis=1).reshape(num_blocks, block_rows, num_experts)
    earlier = (jnp.cumsum(chosen, axis=1) - chosen).reshape(row_count, num_experts)
    position = jnp.sum(matches * earlier[:, None, :], axis=2)
    block_index = (jnp.arange(row_count, dtype=jnp.int32) // block_rows)[:, None]
    return expert_ids * (num_blocks * capacity) + block_index * capacity + position


def reference(activations, out_grad, expert_ids, gate_weights, weight_in, weight_out):
    num_blocks = TOKENS // TOK_DEV
    places = slot_places(expert_ids, num_blocks, CAP, EXPERTS).reshape(-1)
    total_slots = EXPERTS * num_blocks * CAP
    token_index = jnp.broadcast_to(jnp.arange(TOKENS, dtype=jnp.int32)[:, None], (TOKENS, PICKS)).reshape(-1)
    pick_number = jnp.broadcast_to(jnp.arange(PICKS, dtype=jnp.int32)[None, :], (TOKENS, PICKS)).reshape(-1)
    source = jnp.full((total_slots,), TOKENS, jnp.int32).at[places].set(token_index)
    which_pick = jnp.zeros((total_slots,), jnp.int32).at[places].set(pick_number)
    slot_gate = jnp.zeros((total_slots,), jnp.float32).at[places].set(gate_weights.astype(jnp.float32).reshape(-1))
    source = source.reshape(EXPERTS, num_blocks * CAP)
    which_pick = which_pick.reshape(EXPERTS, num_blocks * CAP)
    slot_gate = slot_gate.reshape(EXPERTS, num_blocks * CAP)
    padded_in = jnp.concatenate([activations, jnp.zeros((1, D), jnp.bfloat16)], axis=0)
    padded_grad = jnp.concatenate([out_grad, jnp.zeros((1, D), jnp.bfloat16)], axis=0)

    def one_expert(carry, pieces):
        grad_acc, gate_acc = carry
        chosen_rows, chosen_picks, chosen_gates, first_weight, second_weight = pieces
        inputs = padded_in[chosen_rows]
        grad_rows = padded_grad[chosen_rows]
        before_act = jnp.dot(inputs, first_weight, preferred_element_type=jnp.float32)
        normal_cdf = 0.5 * (1.0 + lax.erf(before_act * ROOT_HALF))
        activated = (before_act * normal_cdf).astype(jnp.bfloat16)
        derivative = normal_cdf + before_act * INV_ROOT_TAU * jnp.exp(-0.5 * before_act * before_act)
        expert_out = jnp.dot(activated, second_weight, preferred_element_type=jnp.float32)
        scores = jnp.sum(expert_out * grad_rows.astype(jnp.float32), axis=-1)
        scaled = (chosen_gates[:, None] * grad_rows.astype(jnp.float32)).astype(jnp.bfloat16)
        grad_act = jnp.dot(scaled, second_weight.T, preferred_element_type=jnp.float32)
        grad_pre = (grad_act * derivative).astype(jnp.bfloat16)
        grad_w_out = jnp.dot(activated.T, scaled, preferred_element_type=jnp.float32).astype(jnp.bfloat16)
        shard_pre = grad_pre.astype(jnp.float32).reshape(-1, N_TENSOR, FF // N_TENSOR)
        shard_weight = first_weight.astype(jnp.float32).reshape(D, N_TENSOR, FF // N_TENSOR)
        partial_value = jnp.einsum("rtf,dtf->trd", shard_pre, shard_weight, precision=lax.Precision.HIGHEST).astype(jnp.bfloat16)
        partial_value = lax.optimization_barrier(partial_value)
        summed = jnp.sum(partial_value.astype(jnp.float32), axis=0)
        grad_acc = grad_acc.at[chosen_rows].add(summed)
        gate_acc = gate_acc.at[chosen_rows, chosen_picks].add(scores)
        return (grad_acc, gate_acc), grad_w_out

    start = (jnp.zeros((TOKENS + 1, D), jnp.float32), jnp.zeros((TOKENS + 1, PICKS), jnp.float32))
    finals, stacked = lax.scan(one_expert, start, (source, which_pick, slot_gate, weight_in, weight_out))
    grad_acc, gate_acc = finals
    return grad_acc[:TOKENS].astype(jnp.bfloat16), gate_acc[:TOKENS], stacked
```

```python
import jax
import jax.numpy as jnp
from jax import lax
from jax.sharding import PartitionSpec as P

EXPERTS = 64
CAP = 3
ROOT_HALF = 0.7071067811865476
INV_ROOT_TAU = 0.3989422804014327


def own_slots(expert_ids):
    rows = expert_ids.shape[0]
    same = expert_ids[:, None] == expert_ids[None, :]
    before = jnp.arange(rows)[None, :] < jnp.arange(rows)[:, None]
    position = jnp.sum((same & before).astype(jnp.int32), axis=1)
    return expert_ids * CAP + position


def on_device(activations, out_grad, expert_ids, gate_weights, weight_in, weight_out):
    rows, width = activations.shape
    expert_size = lax.axis_size("expert")
    tensor_size = lax.axis_size("tensor")
    first = lax.axis_index("tensor") * rows
    ids = lax.dynamic_slice_in_dim(expert_ids[:, 0], first, rows)
    gates = lax.dynamic_slice_in_dim(gate_weights[:, 0], first, rows).astype(jnp.float32)
    slots = own_slots(ids)
    table = slots[:, None] == jnp.arange(EXPERTS * CAP, dtype=jnp.int32)
    spread = table.astype(jnp.bfloat16)
    scaled = (gates[:, None] * out_grad.astype(jnp.float32)).astype(jnp.bfloat16)

    def dispatch(values):
        packed = jnp.dot(spread.T, values, preferred_element_type=jnp.float32)
        packed = packed.astype(jnp.bfloat16).reshape(expert_size, CAP, width)
        there = lax.all_to_all(packed, "expert", split_axis=0, concat_axis=0, tiled=True)
        there = there.reshape(expert_size * CAP, width)
        return lax.all_gather(there, "tensor", axis=0, tiled=True)

    inputs = dispatch(activations)
    grads = dispatch(scaled)
    w_in, w_out = weight_in[0], weight_out[0]
    pre = jnp.dot(inputs, w_in, preferred_element_type=jnp.float32)
    cdf = 0.5 * (1.0 + lax.erf(pre * ROOT_HALF))
    activated = pre * cdf
    slope = cdf + pre * INV_ROOT_TAU * jnp.exp(-0.5 * pre * pre)
    grad_act = jnp.einsum("rd,fd->rf", grads, w_out, preferred_element_type=jnp.float32)
    activated = activated.astype(jnp.bfloat16)
    scores = jnp.sum(activated.astype(jnp.float32) * grad_act, axis=1)
    grad_pre = (grad_act * slope).astype(jnp.bfloat16)
    grad_w_out = jnp.einsum("rf,rd->fd", activated, grads, preferred_element_type=jnp.float32)
    partial = jnp.einsum("rf,df->rd", grad_pre, w_in, preferred_element_type=jnp.float32)
    partial = partial.astype(jnp.bfloat16)
    mine = lax.psum_scatter(partial, "tensor", scatter_dimension=0, tiled=True)
    back = lax.all_to_all(
        mine.reshape(expert_size, CAP, width), "expert", split_axis=0, concat_axis=0, tiled=True
    )
    my_scores = lax.psum_scatter(scores, "tensor", scatter_dimension=0, tiled=True)
    back_scores = lax.all_to_all(
        my_scores.reshape(expert_size, CAP), "expert", split_axis=0, concat_axis=0, tiled=True
    )
    grad_in = jnp.dot(
        spread, back.reshape(-1, width), preferred_element_type=jnp.float32
    ).astype(jnp.bfloat16)
    grad_gates = jnp.sum(jnp.where(table, back_scores.reshape(1, -1), 0.0), axis=1) / gates
    return (grad_in, grad_gates[:, None], grad_w_out.astype(jnp.bfloat16)[None])


def solution(mesh):
    return jax.shard_map(
        on_device,
        mesh=mesh,
        in_specs=(
            P(("expert", "tensor"), None),
            P(("expert", "tensor"), None),
            P("expert", None),
            P("expert", None),
            P("expert", None, "tensor"),
            P("expert", "tensor", None),
        ),
        out_specs=(
            P(("expert", "tensor"), None),
            P(("expert", "tensor"), None),
            P("expert", "tensor", None),
        ),
        check_vma=False,
    )
```

```python
import functools

import jax
import jax.numpy as jnp
from jax import lax
from jax.experimental import pallas as pl
from jax.experimental.pallas import tpu as pltpu
from jax.sharding import PartitionSpec as P

EXPERTS = 64
CAP = 3
ROOT_HALF = 0.7071067811865476
INV_ROOT_TAU = 0.3989422804014327


def slot_positions(expert_ids):
    rows = expert_ids.shape[0]
    same = expert_ids[:, None] == expert_ids[None, :]
    before = jnp.arange(rows)[None, :] < jnp.arange(rows)[:, None]
    return jnp.sum((same & before).astype(jnp.int32), axis=1)


def shift(value, step):
    size = lax.axis_size("tensor")
    return lax.ppermute(value, "tensor", [(i, (i + step) % size) for i in range(size)])


def ring_gather(upper, lower):
    left_u, right_l = shift(upper, 1), shift(lower, -1)
    left_l, right_u = shift(lower, 1), shift(upper, -1)
    far_u, far_l = shift(left_u, 1), shift(right_l, -1)
    return (upper, lower, left_u, left_l, right_u, right_l, far_u, far_l), (left_u, right_l, left_l, right_u)


def after(value, *others):
    return lax.optimization_barrier((value, others))[0]


HBM = pl.BlockSpec(memory_space=pltpu.HBM)
PARAMS = pltpu.CompilerParams(vmem_limit_bytes=60 << 20)
TRANSPOSED = (((1,), (1,)), ((), ()))


def start_all(copies):
    for copy in copies:
        copy.start()


def wait_all(copies):
    for copy in copies:
        copy.wait()


def grad_act_kernel(*refs):
    grads, w_out, out = refs[0:8], refs[8], refs[9]
    rows, w_out_v, sems = refs[10:]
    n = grads[0].shape[0]
    copies = [pltpu.make_async_copy(grads[i], rows.at[pl.ds(i * n, n)], sems.at[i]) for i in range(8)]
    copies.append(pltpu.make_async_copy(w_out, w_out_v, sems.at[8]))
    start_all(copies)
    wait_all(copies)
    step = 2 * n

    def block(i, carry):
        here = pl.ds(pl.multiple_of(i * step, step), step)
        out[here] = lax.dot_general(rows[here], w_out_v[...], TRANSPOSED, preferred_element_type=jnp.float32)
        return carry

    lax.fori_loop(0, 4, block, 0)


def grad_act(grads, w_out):
    n, width = grads[0].shape
    hidden = w_out.shape[0]
    return pl.pallas_call(
        grad_act_kernel,
        out_shape=jax.ShapeDtypeStruct((8 * n, hidden), jnp.float32),
        in_specs=[HBM] * 9,
        scratch_shapes=[
            pltpu.VMEM((8 * n, width), jnp.bfloat16),
            pltpu.VMEM(w_out.shape, jnp.bfloat16),
            pltpu.SemaphoreType.DMA((9,)),
        ],
        compiler_params=PARAMS,
        name="grad_act",
    )(*grads, w_out)


def expert_kernel(slot, *refs):
    tokens, w_in, grad_act_ref = refs[0:4], refs[4], refs[5]
    refs = refs[6:]
    activated_ref, partials = refs[0], refs[1:5]
    rows, w_in_v, act_v, result, sems, out_sems = refs[5:]
    n, width = tokens[0].shape
    half = n // 2
    block = grad_act_ref.shape[0] // 4
    copies = [pltpu.make_async_copy(w_in, w_in_v, sems.at[8])]
    copies += [pltpu.make_async_copy(tokens[i], rows.at[pl.ds(i * n, n)], sems.at[i]) for i in range(4)]
    copies += [
        pltpu.make_async_copy(
            grad_act_ref.at[pl.ds(i * block + slot * n, n)], act_v.at[pl.ds(i * n, n)], sems.at[9 + i]
        )
        for i in range(4)
    ]
    start_all(copies)
    wait_all(copies)
    pre = jnp.dot(rows[...], w_in_v[...], preferred_element_type=jnp.float32)
    cdf = 0.5 * (1.0 + lax.erf(pre * ROOT_HALF))
    slope = cdf + pre * INV_ROOT_TAU * jnp.exp(-0.5 * pre * pre)
    activated = (pre * cdf).astype(jnp.bfloat16)
    activated_ref[...] = activated
    grad = act_v[...]
    score = jnp.sum(activated.astype(jnp.float32) * grad, axis=1, keepdims=True)
    result[:, width:] = jnp.broadcast_to(score, (4 * n, 128)).astype(jnp.bfloat16)
    grad_pre = (grad * slope).astype(jnp.bfloat16)
    stores = []
    for pair in (1, 0):
        rows_of = slice(pair * 2 * n, (pair + 1) * 2 * n)
        part = lax.dot_general(grad_pre[rows_of], w_in_v[...], TRANSPOSED, preferred_element_type=jnp.float32)
        result[rows_of, :width] = part.astype(jnp.bfloat16)
        for i in (2 * pair, 2 * pair + 1):
            stores.append(pltpu.make_async_copy(result.at[pl.ds(i * n, n)], partials[i], out_sems.at[i]))
            stores[-1].start()
    wait_all(stores)


def expert_math(slot, tokens, grad_acts, w_in):
    half, width = tokens[0].shape[0] // 2, tokens[0].shape[1]
    hidden = w_in.shape[1]
    bf16 = jnp.bfloat16
    outs = pl.pallas_call(
        functools.partial(expert_kernel, slot),
        out_shape=[jax.ShapeDtypeStruct((8 * half, hidden), bf16)]
        + [jax.ShapeDtypeStruct((2 * half, width + 128), bf16)] * 4,
        in_specs=[HBM] * 6,
        out_specs=[pl.BlockSpec(memory_space=pltpu.VMEM)] + [HBM] * 4,
        scratch_shapes=[
            pltpu.VMEM((8 * half, width), bf16),
            pltpu.VMEM(w_in.shape, bf16),
            pltpu.VMEM((8 * half, hidden), jnp.float32),
            pltpu.VMEM((8 * half, width + 128), bf16),
            pltpu.SemaphoreType.DMA((13,)),
            pltpu.SemaphoreType.DMA((4,)),
        ],
        compiler_params=PARAMS,
        name="expert",
    )(*tokens, w_in, grad_acts)
    return outs[0], outs[1:]


def weight_grad_kernel(*refs):
    acts, grads = refs[0:CAP], refs[CAP : CAP + 8]
    out, act_rows, grad_rows, a_sems, g_sems = refs[CAP + 8 :]
    n, m = acts[0].shape[0] // 4, grads[0].shape[0]

    @pl.when(pl.program_id(0) == 0)
    def _():
        copies = [
            pltpu.make_async_copy(
                acts[k].at[pl.ds(i * n, n)], act_rows.at[pl.ds((i * CAP + k) * n, n)], a_sems.at[i * CAP + k]
            )
            for i in range(4)
            for k in range(CAP)
        ]
        copies += [pltpu.make_async_copy(grads[i], grad_rows.at[pl.ds(i * m, m)], g_sems.at[i]) for i in range(8)]
        start_all(copies)
        wait_all(copies)

    columns = out.shape[1]
    start = pl.multiple_of(pl.program_id(0) * columns, columns)
    out[...] = lax.dot_general(
        act_rows[...],
        grad_rows[:, pl.ds(start, columns)],
        (((0,), (0,)), ((), ())),
        preferred_element_type=jnp.float32,
    ).astype(jnp.bfloat16)


def weight_grad(acts, grads):
    (n, hidden), (m, width) = acts[0].shape, grads[0].shape
    bf16 = jnp.bfloat16
    return pl.pallas_call(
        weight_grad_kernel,
        grid=(8,),
        out_shape=jax.ShapeDtypeStruct((hidden, width), bf16),
        in_specs=[HBM] * (CAP + 8),
        out_specs=pl.BlockSpec((hidden, width // 8), lambda i: (0, i)),
        scratch_shapes=[
            pltpu.VMEM((CAP * n, hidden), bf16),
            pltpu.VMEM((8 * m, width), bf16),
            pltpu.SemaphoreType.DMA((4 * CAP,)),
            pltpu.SemaphoreType.DMA((8,)),
        ],
        compiler_params=PARAMS,
        name="weight_grad",
    )(*acts, *grads)


def on_device(activations, out_grad, expert_ids, gate_weights, weight_in, weight_out):
    rows, width = activations.shape
    experts = lax.axis_size("expert")
    blocks = width // 128
    first = lax.axis_index("tensor") * rows
    ids = lax.dynamic_slice_in_dim(expert_ids[:, 0], first, rows)
    gates = lax.dynamic_slice_in_dim(gate_weights[:, 0], first, rows).astype(jnp.float32)
    slots = ids * CAP + slot_positions(ids)
    table = (slots[:, None] == jnp.arange(EXPERTS * CAP, dtype=jnp.int32)).astype(jnp.bfloat16)
    scaled = (gates[:, None] * out_grad.astype(jnp.float32)).astype(jnp.bfloat16)
    w_in, w_out = weight_in[0], weight_out[0]

    def exchange(value):
        return lax.all_to_all(value, "expert", split_axis=0, concat_axis=0, tiled=True)

    def pack(values):
        packed = jnp.dot(table.T, values, preferred_element_type=jnp.float32)
        return packed.astype(jnp.bfloat16).reshape(experts, CAP * blocks, 128)

    def by_slot(there, k):
        return there[:, k * blocks : (k + 1) * blocks].reshape(experts, width)

    there = exchange(pack(scaled))
    mine = jnp.concatenate([by_slot(there, k) for k in range(CAP)], axis=0)
    half = mine.shape[0] // 2
    grads, hops = ring_gather(mine[:half], mine[half:])
    there = after(exchange(pack(activations)), hops)
    there = after(there, grads)
    grad_acts = grad_act(grads, w_out)
    acts, backs, sums = [], [], []
    for k in range(CAP):
        mine = by_slot(there, k)
        if k > 0:
            mine = after(mine, hops, grad_acts)
        tokens = (mine, shift(mine, 1), shift(mine, -1), shift(mine, 2))
        hops = tokens[1:3]
        if k == 2:
            tokens = after(tokens, sums[0])
        activated, (own, left, right, far) = expert_math(k, tokens, grad_acts, w_in)
        acts.append(activated)
        parts = [own, shift(far, 2), shift(left, -1), shift(right, 1)]
        if k == 2:
            parts = after(parts, backs[0])
        mine = sum(part.astype(jnp.float32) for part in parts).astype(own.dtype)
        if k == CAP - 1:
            mine, acts[0] = lax.optimization_barrier((mine, acts[0]))
        sums.append(mine)
        backs.append(exchange(mine.reshape(experts, blocks + 1, 128)).reshape(experts, width + 128))
    grad_w_out = weight_grad(acts, grads)
    spreads = [(slots[:, None] == jnp.arange(EXPERTS) * CAP + k).astype(jnp.bfloat16) for k in range(CAP)]
    both = sum(jnp.dot(spreads[k], backs[k], preferred_element_type=jnp.float32) for k in range(CAP))
    grad_gates = (both[:, width] / gates)[:, None]
    return (both[:, :width].astype(jnp.bfloat16), grad_gates, grad_w_out[None])


def solution(mesh):
    return jax.shard_map(
        on_device,
        mesh=mesh,
        in_specs=(
            P(("expert", "tensor"), None),
            P(("expert", "tensor"), None),
            P("expert", None),
            P("expert", None),
            P("expert", None, "tensor"),
            P("expert", "tensor", None),
        ),
        out_specs=(
            P(("expert", "tensor"), None),
            P(("expert", "tensor"), None),
            P("expert", "tensor", None),
        ),
        check_vma=False,
    )
```

```python
import functools

import jax
import jax.numpy as jnp
from jax import lax
from jax.experimental import pallas as pl
from jax.experimental.pallas import tpu as pltpu
from jax.sharding import PartitionSpec as P

EXPERTS = 64
CAP = 3
ROOT_HALF = 0.7071067811865476
INV_ROOT_TAU = 0.3989422804014327


def slot_positions(expert_ids):
    rows = expert_ids.shape[0]
    same = expert_ids[:, None] == expert_ids[None, :]
    before = jnp.arange(rows)[None, :] < jnp.arange(rows)[:, None]
    return jnp.sum((same & before).astype(jnp.int32), axis=1)


def shift(value, step):
    size = lax.axis_size("tensor")
    return lax.ppermute(value, "tensor", [(i, (i + step) % size) for i in range(size)])


def ring_gather(upper, lower):
    left_u, right_l = shift(upper, 1), shift(lower, -1)
    left_l, right_u = shift(lower, 1), shift(upper, -1)
    far_u, far_l = shift(left_u, 1), shift(right_l, -1)
    return (upper, lower, left_u, left_l, right_u, right_l, far_u, far_l), (left_u, right_l, left_l, right_u)


def after(value, *others):
    return lax.optimization_barrier((value, others))[0]


HBM = pl.BlockSpec(memory_space=pltpu.HBM)
PARAMS = pltpu.CompilerParams(vmem_limit_bytes=60 << 20)
TRANSPOSED = (((1,), (1,)), ((), ()))


def start_all(copies):
    for copy in copies:
        copy.start()


def wait_all(copies):
    for copy in copies:
        copy.wait()


def expert_kernel(begin, count, *refs):
    place, tokens, grads = refs[0], refs[1], refs[2 : 2 + count]
    w_in, w_out, activated_ref = refs[2 + count : 5 + count]
    partials = refs[5 + count : 9 + count]
    rows, grad_rows, w_in_v, w_out_v, result, sems, grad_sems, out_sems = refs[9 + count :]
    piece, width = grads[0].shape
    n = piece * count // 4
    block = tokens.shape[0] // 4
    me = place[0]
    owners = (me, lax.rem(me + 3, 4), lax.rem(me + 1, 4), lax.rem(me + 2, 4))
    first = [pltpu.make_async_copy(w_in, w_in_v, sems.at[4])]
    for i in range(4):
        start = pl.multiple_of(owners[i] * block + begin, 64)
        first.append(pltpu.make_async_copy(tokens.at[pl.ds(start, n)], rows.at[pl.ds(i * n, n)], sems.at[i]))
    second = [pltpu.make_async_copy(w_out, w_out_v, sems.at[5])]
    for i in range(count):
        target = grad_rows.at[pl.ds(i * piece, piece)]
        second.append(pltpu.make_async_copy(grads[i], target, grad_sems.at[i]))
    start_all(first + second)
    wait_all(first)
    pre = jnp.dot(rows[...], w_in_v[...], preferred_element_type=jnp.float32)
    cdf = 0.5 * (1.0 + lax.erf(pre * ROOT_HALF))
    slope = cdf + pre * INV_ROOT_TAU * jnp.exp(-0.5 * pre * pre)
    activated = (pre * cdf).astype(jnp.bfloat16)
    activated_ref[...] = activated
    wait_all(second)
    grad = lax.dot_general(grad_rows[...], w_out_v[...], TRANSPOSED, preferred_element_type=jnp.float32)
    score = jnp.sum(activated.astype(jnp.float32) * grad, axis=1, keepdims=True)
    result[:, width:] = jnp.broadcast_to(score, (4 * n, 128)).astype(jnp.bfloat16)
    grad_pre = (grad * slope).astype(jnp.bfloat16)
    stores = []
    for pair in (1, 0):
        rows_of = slice(pair * 2 * n, (pair + 1) * 2 * n)
        part = lax.dot_general(grad_pre[rows_of], w_in_v[...], TRANSPOSED, preferred_element_type=jnp.float32)
        result[rows_of, :width] = part.astype(jnp.bfloat16)
        for i in (2 * pair, 2 * pair + 1):
            stores.append(pltpu.make_async_copy(result.at[pl.ds(i * n, n)], partials[i], out_sems.at[i]))
            stores[-1].start()
    wait_all(stores)


def expert_math(begin, place, tokens, grads, w_in, w_out):
    count, (piece, width) = len(grads), grads[0].shape
    n = piece * count // 4
    hidden = w_in.shape[1]
    bf16 = jnp.bfloat16
    outs = pl.pallas_call(
        functools.partial(expert_kernel, begin, count),
        out_shape=[jax.ShapeDtypeStruct((4 * n, hidden), bf16)]
        + [jax.ShapeDtypeStruct((n, width + 128), bf16)] * 4,
        in_specs=[pl.BlockSpec(memory_space=pltpu.SMEM)] + [HBM] * (3 + count),
        out_specs=[pl.BlockSpec(memory_space=pltpu.VMEM)] + [HBM] * 4,
        scratch_shapes=[
            pltpu.VMEM((4 * n, width), bf16),
            pltpu.VMEM((4 * n, width), bf16),
            pltpu.VMEM(w_in.shape, bf16),
            pltpu.VMEM(w_out.shape, bf16),
            pltpu.VMEM((4 * n, width + 128), bf16),
            pltpu.SemaphoreType.DMA((6,)),
            pltpu.SemaphoreType.DMA((8,)),
            pltpu.SemaphoreType.DMA((4,)),
        ],
        compiler_params=PARAMS,
        name="expert",
    )(place, tokens, *grads, w_in, w_out)
    return outs[0], outs[1:]


def weight_grad_kernel(counts, *refs):
    parts = len(counts)
    acts, grads = refs[0:parts], refs[parts : parts + sum(counts)]
    out, act_rows, grad_rows, a_sems, g_sems = refs[parts + sum(counts) :]
    block = act_rows.shape[0] // 4

    @pl.when(pl.program_id(0) == 0)
    def _():
        copies, begin, number = [], 0, 0
        for k in range(parts):
            n = acts[k].shape[0] // 4
            for i in range(4):
                target = act_rows.at[pl.ds(i * block + begin, n)]
                copies.append(pltpu.make_async_copy(acts[k].at[pl.ds(i * n, n)], target, a_sems.at[4 * k + i]))
            each = counts[k] // 4
            for i in range(counts[k]):
                piece = n // each
                target = grad_rows.at[pl.ds(i // each * block + begin + i % each * piece, piece)]
                copies.append(pltpu.make_async_copy(grads[number + i], target, g_sems.at[number + i]))
            begin, number = begin + n, number + counts[k]
        start_all(copies)
        wait_all(copies)

    columns = out.shape[1]
    start = pl.multiple_of(pl.program_id(0) * columns, columns)
    out[...] = lax.dot_general(
        act_rows[...],
        grad_rows[:, pl.ds(start, columns)],
        (((0,), (0,)), ((), ())),
        preferred_element_type=jnp.float32,
    ).astype(jnp.bfloat16)


def weight_grad(acts, grads):
    hidden, width = acts[0].shape[1], grads[0][0].shape[1]
    rows = sum(act.shape[0] for act in acts)
    counts = tuple(len(pieces) for pieces in grads)
    bf16 = jnp.bfloat16
    return pl.pallas_call(
        functools.partial(weight_grad_kernel, counts),
        grid=(8,),
        out_shape=jax.ShapeDtypeStruct((hidden, width), bf16),
        in_specs=[HBM] * (len(acts) + sum(counts)),
        out_specs=pl.BlockSpec((hidden, width // 8), lambda i: (0, i)),
        scratch_shapes=[
            pltpu.VMEM((rows, hidden), bf16),
            pltpu.VMEM((rows, width), bf16),
            pltpu.SemaphoreType.DMA((4 * len(acts),)),
            pltpu.SemaphoreType.DMA((sum(counts),)),
        ],
        compiler_params=PARAMS,
        name="weight_grad",
    )(*acts, *[piece for pieces in grads for piece in pieces])


def on_device(activations, out_grad, expert_ids, gate_weights, weight_in, weight_out):
    rows, width = activations.shape
    experts = lax.axis_size("expert")
    blocks = width // 128
    first = lax.axis_index("tensor") * rows
    ids = lax.dynamic_slice_in_dim(expert_ids[:, 0], first, rows)
    gates = lax.dynamic_slice_in_dim(gate_weights[:, 0], first, rows).astype(jnp.float32)
    slots = ids * CAP + slot_positions(ids)
    table = (slots[:, None] == jnp.arange(EXPERTS * CAP, dtype=jnp.int32)).astype(jnp.bfloat16)
    scaled = (gates[:, None] * out_grad.astype(jnp.float32)).astype(jnp.bfloat16)
    w_in, w_out = weight_in[0], weight_out[0]

    def exchange(value):
        return lax.all_to_all(value, "expert", split_axis=0, concat_axis=0, tiled=True)

    def pack(values):
        packed = jnp.dot(table.T, values, preferred_element_type=jnp.float32)
        return packed.astype(jnp.bfloat16).reshape(experts, CAP * blocks, 128)

    def by_slot(there, k):
        return there[:, k * blocks : (k + 1) * blocks].reshape(experts, width)

    packed, sent = lax.optimization_barrier((pack(activations), pack(scaled)))
    last = sent[:, (CAP - 1) * blocks :]
    early = (last, shift(last, 1), shift(last, -1), shift(last, 2))
    there = exchange(packed)
    mine = after(jnp.concatenate([by_slot(there, k) for k in range(CAP)], axis=0), early)
    tokens = lax.all_gather(mine, "tensor", axis=0, tiled=True)
    there = exchange(after(sent[:, : (CAP - 1) * blocks], early, there))
    whole = exchange(after(jnp.concatenate(early, axis=1), there))
    ring, _ = ring_gather(by_slot(there, 0), by_slot(there, 1))
    grads = [ring]
    place = lax.axis_index("tensor").reshape(1)
    acts, parts, sums = [], [], []
    for turn in range(2):
        begin = turn * (CAP - 1) * experts
        if turn == 1:
            grads.append(tuple(by_slot(after(whole, acts[0]), i) for i in range(4)))
        activated, (own, left, right, far) = expert_math(begin, place, tokens, grads[turn], w_in, w_out)
        acts.append(activated)
        parts.append([own, shift(far, 2), shift(left, -1), shift(right, 1)])
    parts[0] = after(parts[0], acts[1])
    for turn in range(2):
        if turn == 1:
            pair = jnp.concatenate([sums[0][:experts, :width], sums[0][experts:, :width]], axis=1)
            back = exchange(pair.reshape(experts, 2 * blocks, 128))
        sums.append(sum(part.astype(jnp.float32) for part in parts[turn]).astype(jnp.bfloat16))
    slotwise = [sums[0][:experts], sums[0][experts:], sums[1]]
    rest = [sums[1][:, :width]] + [part[:, width:] for part in slotwise]
    rest, acts[0], back = lax.optimization_barrier((jnp.concatenate(rest, axis=1), acts[0], back))
    rest = exchange(rest.reshape(experts, -1, 128)).reshape(experts, -1)
    back = back.reshape(experts, 2 * width)
    backs = [back[:, :width], back[:, width:], rest[:, :width]]
    chosen = [rest[:, width + 128 * k : width + 128 * (k + 1)] for k in range(CAP)]
    grad_w_out = weight_grad(acts, grads)
    spreads = [(slots[:, None] == jnp.arange(EXPERTS) * CAP + k).astype(jnp.bfloat16) for k in range(CAP)]
    grad_in = sum(jnp.dot(spreads[k], backs[k], preferred_element_type=jnp.float32) for k in range(CAP))
    chosen = sum(jnp.dot(spreads[k], chosen[k], preferred_element_type=jnp.float32) for k in range(CAP))
    grad_gates = (chosen[:, 0] / gates)[:, None]
    return (grad_in.astype(jnp.bfloat16), grad_gates, grad_w_out[None])


def solution(mesh):
    return jax.shard_map(
        on_device,
        mesh=mesh,
        in_specs=(
            P(("expert", "tensor"), None),
            P(("expert", "tensor"), None),
            P("expert", None),
            P("expert", None),
            P("expert", None, "tensor"),
            P("expert", "tensor", None),
        ),
        out_specs=(
            P(("expert", "tensor"), None),
            P(("expert", "tensor"), None),
            P("expert", "tensor", None),
        ),
        check_vma=False,
    )
```

```python
import functools

import jax
import jax.numpy as jnp
from jax import lax
from jax.experimental import pallas as pl
from jax.experimental.pallas import tpu as pltpu
from jax.sharding import PartitionSpec as P

EXPERTS = 64
CAP = 3
ROOT_HALF = 0.7071067811865476
INV_ROOT_TAU = 0.3989422804014327


def slot_positions(expert_ids):
    rows = expert_ids.shape[0]
    same = expert_ids[:, None] == expert_ids[None, :]
    before = jnp.arange(rows)[None, :] < jnp.arange(rows)[:, None]
    return jnp.sum((same & before).astype(jnp.int32), axis=1)


def shift(value, step):
    size = lax.axis_size("tensor")
    return lax.ppermute(value, "tensor", [(i, (i + step) % size) for i in range(size)])


def ring_gather(upper, lower):
    left_u, right_l = shift(upper, 1), shift(lower, -1)
    left_l, right_u = shift(lower, 1), shift(upper, -1)
    far_u, far_l = shift(left_u, 1), shift(right_l, -1)
    return (upper, lower, left_u, left_l, right_u, right_l, far_u, far_l), (left_u, right_l, left_l, right_u)


def after(value, *others):
    return lax.optimization_barrier((value, others))[0]


HBM = pl.BlockSpec(memory_space=pltpu.HBM)
PARAMS = pltpu.CompilerParams(vmem_limit_bytes=60 << 20)
TRANSPOSED = (((1,), (1,)), ((), ()))


def start_all(copies):
    for copy in copies:
        copy.start()


def wait_all(copies):
    for copy in copies:
        copy.wait()


def expert_kernel(begin, count, *refs):
    place, tokens, grads = refs[0], refs[1], refs[2 : 2 + count]
    w_in, w_out, activated_ref = refs[2 + count : 5 + count]
    split = count // 4
    partials = refs[5 + count : 5 + 2 * count]
    rows, grad_rows, w_in_v, w_out_v, result, sems, grad_sems, out_sems = refs[5 + 2 * count :]
    piece, width = grads[0].shape
    n = piece * count // 4
    block = tokens.shape[0] // 4
    me = place[0]
    owners = (me, lax.rem(me + 3, 4), lax.rem(me + 1, 4), lax.rem(me + 2, 4))
    first = [pltpu.make_async_copy(w_in, w_in_v, sems.at[4])]
    for i in range(4):
        start = pl.multiple_of(owners[i] * block + begin, 64)
        first.append(pltpu.make_async_copy(tokens.at[pl.ds(start, n)], rows.at[pl.ds(i * n, n)], sems.at[i]))
    second = [pltpu.make_async_copy(w_out, w_out_v, sems.at[5])]
    for i in range(count):
        target = grad_rows.at[pl.ds(i * piece, piece)]
        second.append(pltpu.make_async_copy(grads[i], target, grad_sems.at[i]))
    start_all(first + second)
    wait_all(first)
    pre = jnp.dot(rows[...], w_in_v[...], preferred_element_type=jnp.float32)
    cdf = 0.5 * (1.0 + lax.erf(pre * ROOT_HALF))
    slope = cdf + pre * INV_ROOT_TAU * jnp.exp(-0.5 * pre * pre)
    activated = (pre * cdf).astype(jnp.bfloat16)
    activated_ref[...] = activated
    wait_all(second)
    grad = lax.dot_general(grad_rows[...], w_out_v[...], TRANSPOSED, preferred_element_type=jnp.float32)
    score = jnp.sum(activated.astype(jnp.float32) * grad, axis=1, keepdims=True)
    result[:, width:] = jnp.broadcast_to(score, (4 * n, 128)).astype(jnp.bfloat16)
    grad_pre = (grad * slope).astype(jnp.bfloat16)
    stores = []
    for pair in (1, 0):
        rows_of = slice(pair * 2 * n, (pair + 1) * 2 * n)
        part = lax.dot_general(grad_pre[rows_of], w_in_v[...], TRANSPOSED, preferred_element_type=jnp.float32)
        result[rows_of, :width] = part.astype(jnp.bfloat16)
        for i in range(2 * pair * split, 2 * (pair + 1) * split):
            stores.append(pltpu.make_async_copy(result.at[pl.ds(i * piece, piece)], partials[i], out_sems.at[i]))
            stores[-1].start()
    wait_all(stores)


def expert_math(begin, place, tokens, grads, w_in, w_out):
    count, (piece, width) = len(grads), grads[0].shape
    n = piece * count // 4
    hidden = w_in.shape[1]
    bf16 = jnp.bfloat16
    outs = pl.pallas_call(
        functools.partial(expert_kernel, begin, count),
        out_shape=[jax.ShapeDtypeStruct((4 * n, hidden), bf16)]
        + [jax.ShapeDtypeStruct((piece, width + 128), bf16)] * count,
        in_specs=[pl.BlockSpec(memory_space=pltpu.SMEM)] + [HBM] * (3 + count),
        out_specs=[pl.BlockSpec(memory_space=pltpu.VMEM)] + [HBM] * count,
        scratch_shapes=[
            pltpu.VMEM((4 * n, width), bf16),
            pltpu.VMEM((4 * n, width), bf16),
            pltpu.VMEM(w_in.shape, bf16),
            pltpu.VMEM(w_out.shape, bf16),
            pltpu.VMEM((4 * n, width + 128), bf16),
            pltpu.SemaphoreType.DMA((6,)),
            pltpu.SemaphoreType.DMA((8,)),
            pltpu.SemaphoreType.DMA((8,)),
        ],
        compiler_params=PARAMS,
        name="expert",
    )(place, tokens, *grads, w_in, w_out)
    return outs[0], outs[1:]


def weight_grad_kernel(counts, *refs):
    parts = len(counts)
    acts, grads = refs[0:parts], refs[parts : parts + sum(counts)]
    out, act_rows, grad_rows, a_sems, g_sems = refs[parts + sum(counts) :]
    block = act_rows.shape[0] // 4

    @pl.when(pl.program_id(0) == 0)
    def _():
        copies, begin, number = [], 0, 0
        for k in range(parts):
            n = acts[k].shape[0] // 4
            for i in range(4):
                target = act_rows.at[pl.ds(i * block + begin, n)]
                copies.append(pltpu.make_async_copy(acts[k].at[pl.ds(i * n, n)], target, a_sems.at[4 * k + i]))
            each = counts[k] // 4
            for i in range(counts[k]):
                piece = n // each
                target = grad_rows.at[pl.ds(i // each * block + begin + i % each * piece, piece)]
                copies.append(pltpu.make_async_copy(grads[number + i], target, g_sems.at[number + i]))
            begin, number = begin + n, number + counts[k]
        start_all(copies)
        wait_all(copies)

    columns = out.shape[1]
    start = pl.multiple_of(pl.program_id(0) * columns, columns)
    out[...] = lax.dot_general(
        act_rows[...],
        grad_rows[:, pl.ds(start, columns)],
        (((0,), (0,)), ((), ())),
        preferred_element_type=jnp.float32,
    ).astype(jnp.bfloat16)


def weight_grad(acts, grads):
    hidden, width = acts[0].shape[1], grads[0][0].shape[1]
    rows = sum(act.shape[0] for act in acts)
    counts = tuple(len(pieces) for pieces in grads)
    bf16 = jnp.bfloat16
    return pl.pallas_call(
        functools.partial(weight_grad_kernel, counts),
        grid=(8,),
        out_shape=jax.ShapeDtypeStruct((hidden, width), bf16),
        in_specs=[HBM] * (len(acts) + sum(counts)),
        out_specs=pl.BlockSpec((hidden, width // 8), lambda i: (0, i)),
        scratch_shapes=[
            pltpu.VMEM((rows, hidden), bf16),
            pltpu.VMEM((rows, width), bf16),
            pltpu.SemaphoreType.DMA((4 * len(acts),)),
            pltpu.SemaphoreType.DMA((sum(counts),)),
        ],
        compiler_params=PARAMS,
        name="weight_grad",
    )(*acts, *[piece for pieces in grads for piece in pieces])


def on_device(activations, out_grad, expert_ids, gate_weights, weight_in, weight_out):
    rows, width = activations.shape
    experts = lax.axis_size("expert")
    blocks = width // 128
    first = lax.axis_index("tensor") * rows
    ids = lax.dynamic_slice_in_dim(expert_ids[:, 0], first, rows)
    gates = lax.dynamic_slice_in_dim(gate_weights[:, 0], first, rows).astype(jnp.float32)
    slots = ids * CAP + slot_positions(ids)
    table = (slots[:, None] == jnp.arange(EXPERTS * CAP, dtype=jnp.int32)).astype(jnp.bfloat16)
    scaled = (gates[:, None] * out_grad.astype(jnp.float32)).astype(jnp.bfloat16)
    w_in, w_out = weight_in[0], weight_out[0]

    def exchange(value):
        return lax.all_to_all(value, "expert", split_axis=0, concat_axis=0, tiled=True)

    def pack(values):
        packed = jnp.dot(table.T, values, preferred_element_type=jnp.float32)
        return packed.astype(jnp.bfloat16).reshape(experts, CAP * blocks, 128)

    def by_slot(there, k):
        return there[:, k * blocks : (k + 1) * blocks].reshape(experts, width)

    packed, sent = lax.optimization_barrier((pack(activations), pack(scaled)))
    last = sent[:, (CAP - 1) * blocks :]
    early = (last, shift(last, 1), shift(last, -1), shift(last, 2))
    there = exchange(packed)
    mine = after(jnp.concatenate([by_slot(there, k) for k in range(CAP)], axis=0), early)
    tokens = lax.all_gather(mine, "tensor", axis=0, tiled=True)
    there = exchange(after(sent[:, : (CAP - 1) * blocks], early, there))
    whole = exchange(after(jnp.concatenate(early, axis=1), there))
    ring, _ = ring_gather(by_slot(there, 0), by_slot(there, 1))
    grads = [ring]
    place = lax.axis_index("tensor").reshape(1)
    f32, bf16 = jnp.float32, jnp.bfloat16

    def total(*values):
        return sum(value.astype(f32) for value in values).astype(bf16)

    first, ends = expert_math(0, place, tokens, grads[0], w_in, w_out)
    own, left, right, far = ends[0:2], ends[2:4], ends[4:6], ends[6:8]
    from_left, from_right = shift(far[1], 1), shift(far[0], -1)
    plain_right, plain_left = shift(right[0], 1), shift(left[1], -1)
    pieces = tuple(by_slot(after(whole, first), i) for i in range(4))
    grads.append(pieces)
    second, ends = expert_math((CAP - 1) * experts, place, tokens, pieces, w_in, w_out)
    acts = [first, second]
    from_left, from_right = after((from_left, from_right), second)
    both_right = shift(total(right[1], from_left), 1)
    both_left = shift(total(left[0], from_right), -1)
    lone = [ends[0], shift(ends[3], 2), shift(ends[1], -1), shift(ends[2], 1)]
    upper, lower = total(own[0], plain_right, both_left), total(own[1], both_right, plain_left)
    pair = jnp.concatenate([upper[:, :width], lower[:, :width]], axis=1)
    back = exchange(pair.reshape(experts, 2 * blocks, 128))
    sums = [None, total(*lone)]
    slotwise = [upper, lower, sums[1]]
    rest = [sums[1][:, :width]] + [part[:, width:] for part in slotwise]
    rest, acts[0], back = lax.optimization_barrier((jnp.concatenate(rest, axis=1), acts[0], back))
    rest = exchange(rest.reshape(experts, -1, 128)).reshape(experts, -1)
    back = back.reshape(experts, 2 * width)
    backs = [back[:, :width], back[:, width:], rest[:, :width]]
    chosen = [rest[:, width + 128 * k : width + 128 * (k + 1)] for k in range(CAP)]
    grad_w_out = weight_grad(acts, grads)
    spreads = [(slots[:, None] == jnp.arange(EXPERTS) * CAP + k).astype(jnp.bfloat16) for k in range(CAP)]
    grad_in = sum(jnp.dot(spreads[k], backs[k], preferred_element_type=jnp.float32) for k in range(CAP))
    chosen = sum(jnp.dot(spreads[k], chosen[k], preferred_element_type=jnp.float32) for k in range(CAP))
    grad_gates = (chosen[:, 0] / gates)[:, None]
    return (grad_in.astype(jnp.bfloat16), grad_gates, grad_w_out[None])


def solution(mesh):
    return jax.shard_map(
        on_device,
        mesh=mesh,
        in_specs=(
            P(("expert", "tensor"), None),
            P(("expert", "tensor"), None),
            P("expert", None),
            P("expert", None),
            P("expert", None, "tensor"),
            P("expert", "tensor", None),
        ),
        out_specs=(
            P(("expert", "tensor"), None),
            P(("expert", "tensor"), None),
            P("expert", "tensor", None),
        ),
        check_vma=False,
    )
```
